32 devices in a mesh: chan: 8 (over z, y), grp: 4 (over x, core).
Axes of the slice: x: 2, y: 2, z: 4, core: 2. Of those that a mesh axis runs over, the one named last changes fastest.
Arguments:
- eta_pp: bfloat16 [32, 640, 640], P(('chan', 'grp'))
- ham_pp: bfloat16 [32, 640, 640], P(('chan', 'grp'))
- pp_factor: float32 [32, 640], P(('chan', 'grp')), may hold values from -1 to 1
- ph_factor: float32 [32, 640], P(('chan', 'grp')), may hold values from -1 to 1
- channel_size: int32 [32], P(('chan', 'grp')), may hold values from 320 to 640, as said below
- dest_dev: int32 [32, 160], P(('chan', 'grp')), may hold values from 0 to 7, as said below
- dest_sub: int32 [32, 160], P(('chan', 'grp')), may hold values from 0 to 159, as said below
- col_map: int32 [32, 640], P(('chan', 'grp')), may hold values from 0 to 639, each once within a row
- pair_swap: int32 [32, 640], P(('chan', 'grp')), may hold values from 0 to 639, as said below
Outputs:
- pp_flow: float32 [32, 640, 640], P(('chan', 'grp'))
- energy_flow: float32 [], replicated
The draws below stay inside these ranges and needn't reach their ends.
Inputs may be any that keep to these rules, and one draw needn't show every extreme that they name: `channel_size`: a multiple of 4. `dest_dev`: every ph channel receives each of its 160 positions from exactly one pp subblock of its own group; from one pp channel at most 20 subblocks go to one ph channel, and exactly 20 for some. `dest_sub`: for each ph channel the positions it receives are all different. `pair_swap`: an involution of each channel's pairs without fixed points.
All inputs are finite; a program needn't handle non-finite values.
Results may differ from the reference program's by a relative error of at most 0.0036.
Values may be sent and summed in bfloat16 or wider, within the bound.
No kernel may reach another device: no remote copies, remote signals or barrier semaphores. Data moves between devices by JAX's collectives and lax.ppermute only.
A program may use at most 64 MiB of HBM per device.

```python
import jax
import jax.numpy as jnp
from jax import lax

CAP = 640
STRIP = 4
SUBS = 160
CHANNELS = 32
N_CHAN = 8
N_GRP = 4


def route_tables(key):
    base = jax.random.fold_in(key, 11)
    key_shift, key_label, key_order = jax.random.split(base, 3)
    shifts = jax.vmap(lambda k: jax.random.permutation(k, N_CHAN))(jax.random.split(key_shift, N_GRP))
    labels = jax.vmap(lambda k: jax.random.permutation(k, N_CHAN))(jax.random.split(key_label, N_GRP))
    orders = jax.vmap(lambda k: jax.random.permutation(k, SUBS))(jax.random.split(key_order, N_CHAN * N_GRP))
    orders = orders.reshape(N_CHAN, N_GRP, SUBS)
    source = jnp.arange(N_CHAN, dtype=jnp.int32)[:, None, None]
    group = jnp.arange(N_GRP, dtype=jnp.int32)[None, :, None]
    block = jnp.arange(SUBS, dtype=jnp.int32)[None, None, :]
    offset = shifts[group, block % N_CHAN]
    targets = labels[group, (source + offset) % N_CHAN]
    position = orders[targets, group, block]
    return (targets.reshape(N_CHAN * N_GRP, SUBS).astype(jnp.int32), position.reshape(N_CHAN * N_GRP, SUBS).astype(jnp.int32))


def draw_dest_dev(key, part):
    return route_tables(key)[0]


def draw_dest_sub(key, part):
    return route_tables(key)[1]


def draw_channel_size(key, part):
    inner = jax.random.fold_in(key, 23)
    counts = jax.random.randint(inner, (N_CHAN * N_GRP,), SUBS // 2, SUBS + 1)
    counts = counts.at[0].set(SUBS).at[1].set(SUBS // 2)
    return (STRIP * counts).astype(jnp.int32)


def draw_pair_swap(key, part):
    inner = jax.random.fold_in(key, 37)

    def involution(k):
        shuffled = jax.random.permutation(k, CAP)
        firsts = shuffled[0::2]
        seconds = shuffled[1::2]
        partner = jnp.zeros((CAP,), jnp.int32).at[firsts].set(seconds)
        return partner.at[seconds].set(firsts)
    return jax.vmap(involution)(jax.random.split(inner, N_CHAN * N_GRP)).astype(jnp.int32)


def factor_rows(key):
    inner = jax.random.fold_in(key, 51)
    return jax.random.uniform(inner, (N_CHAN * N_GRP, CAP), jnp.float32, -1.0, 1.0)


def flow_tables(key, which):
    factors = factor_rows(key)
    inner = jax.random.fold_in(key, 53)
    channel_keys = jax.random.split(inner, N_CHAN * N_GRP)

    def one_channel(args):
        k, factor = args
        key_ham, key_mag = jax.random.split(k)
        raw = jax.random.normal(key_ham, (CAP, CAP), jnp.float32)
        ham = (raw + raw.T) / jnp.sqrt(2.0 * CAP)
        spread = jax.random.uniform(key_mag, (CAP, CAP), jnp.float32, 0.5, 1.5)
        spread = 0.5 * (spread + spread.T)
        direction = jnp.sign(factor[None, :] - factor[:, None])
        gen = spread * ham * direction
        if which == 0:
            return gen.astype(jnp.bfloat16)
        return ham.astype(jnp.bfloat16)
    return lax.map(one_channel, (channel_keys, factors))


def draw_pp_factor(key, part):
    return factor_rows(key)


def draw_eta_pp(key, part):
    return flow_tables(key, 0)


def draw_ham_pp(key, part):
    return flow_tables(key, 1)


def levels(key, shape, shards, least, largest):
    level, own = 1.0, jax.random.fold_in(key, 6)
    for dim, parts in shards:
        draws = jnp.exp(jax.random.uniform(jax.random.fold_in(own, dim), (parts,), jnp.float32, least / len(shards), largest / len(shards)))
        level = level * jnp.repeat(draws, shape[dim] // parts).reshape([-1 if axis == dim else 1 for axis in range(len(shape))])
    return level


def setup_inputs(seed: int = 0) -> dict:
    keys = jax.random.split(jax.random.key(seed), 10)
    return {
        "eta_pp": draw_eta_pp(jax.random.fold_in(keys[9], 71), 0),
        "ham_pp": draw_ham_pp(jax.random.fold_in(keys[9], 71), 0),
        "pp_factor": draw_pp_factor(jax.random.fold_in(keys[9], 71), 0),
        "ph_factor": jnp.clip(jax.random.uniform(keys[3], (CHANNELS, CAP), jnp.float32, -1.0, 1.0) * levels(keys[3], (CHANNELS, CAP), ((0, 32),), -0.4, 0.0), -1.0, 1.0),
        "channel_size": draw_channel_size(jax.random.fold_in(keys[9], 71), 0),
        "dest_dev": draw_dest_dev(jax.random.fold_in(keys[9], 71), 0),
        "dest_sub": draw_dest_sub(jax.random.fold_in(keys[9], 71), 0),
        "col_map": jax.vmap(lambda own: jax.random.permutation(own, CAP))(jax.random.split(keys[7], CHANNELS)).reshape((CHANNELS, CAP)).astype(jnp.int32),
        "pair_swap": draw_pair_swap(jax.random.fold_in(keys[9], 71), 0),
    }


def mask_channel(args):
    gen_block, ham_block, size = args
    pair_index = jnp.arange(CAP, dtype=jnp.int32)
    living = pair_index < size
    inside = living[:, None] & living[None, :]
    zero = jnp.zeros((), jnp.bfloat16)
    return jnp.where(inside, gen_block, zero), jnp.where(inside, ham_block, zero)


def product(left, right):
    return jnp.dot(left.astype(jnp.float32), right.astype(jnp.float32), preferred_element_type=jnp.float32)


def ph_channel(args):
    gen_rows, ham_rows, ph_scale, columns = args
    gen_ph = jnp.take(gen_rows.reshape(CAP, CAP), columns, axis=1)
    ham_ph = jnp.take(ham_rows.reshape(CAP, CAP), columns, axis=1)
    scaled_ham = (ph_scale[:, None] * ham_ph.astype(jnp.float32)).astype(jnp.bfloat16)
    scaled_gen = (ph_scale[:, None] * gen_ph.astype(jnp.float32)).astype(jnp.bfloat16)
    commuted = product(gen_ph, scaled_ham) - product(ham_ph, scaled_gen)
    commuted = commuted.astype(jnp.bfloat16)
    unperm = jnp.zeros((CAP, CAP), jnp.bfloat16).at[:, columns].set(commuted)
    return unperm.reshape(SUBS, STRIP * CAP)


def pp_channel(args):
    gen_m, ham_m, pp_scale, back_rows, partner, size = args
    scaled_ham = (pp_scale[:, None] * ham_m.astype(jnp.float32)).astype(jnp.bfloat16)
    scaled_gen = (pp_scale[:, None] * gen_m.astype(jnp.float32)).astype(jnp.bfloat16)
    ladder = product(gen_m, scaled_ham) - product(ham_m, scaled_gen)
    back = back_rows.reshape(CAP, CAP).astype(jnp.float32)
    anti = back - back[partner, :] - back[:, partner] + back[partner, :][:, partner]
    pair_index = jnp.arange(CAP, dtype=jnp.int32)
    living = pair_index < size
    inside = living[:, None] & living[None, :]
    flow = jnp.where(inside, 0.5 * ladder + anti, jnp.zeros((), jnp.float32))
    return flow, jnp.trace(ladder)


def reference(eta_pp, ham_pp, pp_factor, ph_factor, channel_size, dest_dev, dest_sub, col_map, pair_swap):
    chans = eta_pp.shape[0]
    gen_m, ham_m = lax.map(mask_channel, (eta_pp, ham_pp, channel_size))
    group_of = (jnp.arange(chans, dtype=jnp.int32) % N_GRP).astype(jnp.int32)
    targets = (dest_dev * N_GRP + group_of[:, None]).astype(jnp.int32)
    gen_strips = gen_m.reshape(chans, SUBS, STRIP * CAP)
    ham_strips = ham_m.reshape(chans, SUBS, STRIP * CAP)
    raw_gen = jnp.zeros_like(gen_strips).at[targets, dest_sub].set(gen_strips)
    raw_ham = jnp.zeros_like(ham_strips).at[targets, dest_sub].set(ham_strips)
    ph_back = lax.map(ph_channel, (raw_gen, raw_ham, ph_factor, col_map))
    back = ph_back[targets, dest_sub]
    flow, traces = lax.map(pp_channel, (gen_m, ham_m, pp_factor, back, pair_swap, channel_size))
    energy_flow = 0.25 * jnp.sum(traces)
    return flow, energy_flow
```

```python
import functools

import jax
import jax.numpy as jnp
from jax import lax
from jax.experimental import pallas as pl
from jax.experimental.pallas import tpu as pltpu
from jax.sharding import PartitionSpec as P


LANES = 128
MAX_PERMUTE_PEERS = 16
F32 = jnp.float32
BF16 = jnp.bfloat16
VMEM = pl.BlockSpec(memory_space=pltpu.VMEM)
SMEM = pl.BlockSpec(memory_space=pltpu.SMEM)


def iota(shape, dim):
    return lax.broadcasted_iota(jnp.int32, shape, dim)


def iota_f(shape, dim):
    return iota(shape, dim).astype(F32)


def dot(a, b):
    return jnp.dot(a, b, preferred_element_type=F32)


def to_column(row):
    n = row.shape[1]
    same = iota((n, n), 0) == iota((n, n), 1)
    return jnp.sum(jnp.where(same, row, 0.0), axis=1, keepdims=True)


class Plan:
    def __init__(self, cap, subs, peers):
        self.cap = cap
        self.subs = subs
        self.peers = peers
        self.strip = cap // subs
        self.slots = (subs + peers - 1) // peers
        self.slot_rows = peers * self.slots * self.strip
        self.permutes = (
            peers <= MAX_PERMUTE_PEERS
            and peers & (peers - 1) == 0
            and (self.slots * self.strip) % 16 == 0
            and cap % LANES == 0
            and self.slot_rows <= 8 * LANES
            and self.slot_rows % LANES == 0
            and subs + 1 <= 256
        )
        self.blocks = peers if self.permutes else 1
        self.rows = self.slot_rows // self.blocks
        self.tiles = cap // LANES
        self.gen_shape = (
            (self.tiles * self.rows + 8, LANES) if self.permutes else (self.rows, cap)
        )


def pack_gen_kernel(plan, me_ref, size_ref, dev_ref, sub_ref, gen_ref, place_ref, pos_ref, *out_refs):
    subs, cap, strip, slot_rows = plan.subs, plan.cap, plan.strip, plan.slot_rows
    size = size_ref[0]
    target = dev_ref[...]
    if plan.permutes:
        target = target ^ me_ref[0]
    target = target.astype(F32)
    target_col = to_column(target)
    earlier = (target_col == target) & (iota((subs, subs), 1) < iota((subs, subs), 0))
    rank = jnp.sum(jnp.where(earlier, 1.0, 0.0), axis=1, keepdims=True)
    slot_row = (target_col * plan.slots + rank) * strip
    lane = iota_f((subs, cap), 1) - iota_f((subs, cap), 0) * strip
    place = jnp.sum(
        jnp.where((lane >= 0) & (lane < strip), slot_row + lane, 0.0), axis=0, keepdims=True
    )
    place = jnp.where(iota((1, cap), 1) < size, place, -1.0)
    place_ref[...] = place
    sub_col = to_column(sub_ref[...].astype(F32))
    within = iota_f((subs, slot_rows), 1) - slot_row
    pos = jnp.sum(
        jnp.where((within >= 0) & (within < strip), sub_col + 1.0, 0.0), axis=0, keepdims=True
    )
    pos_ref[...] = pos
    send = jnp.where(iota_f((slot_rows, cap), 0) == place, 1.0, 0.0).astype(BF16)
    packed = dot(send, gen_ref[0])
    packed = jnp.where(iota((slot_rows, cap), 1) < size, packed, 0.0).astype(BF16)
    if not plan.permutes:
        out_refs[0][...] = packed
        return
    rows, tiles = plan.rows, plan.tiles
    pos_tile = jnp.zeros((8, LANES), F32)
    slot_lane = jnp.zeros((8, LANES), jnp.int32)
    for t in range(slot_rows // LANES):
        pos_tile = jnp.where(
            iota((8, LANES), 0) == t, pos[:, t * LANES : (t + 1) * LANES], pos_tile
        )
    slot_lane = iota((8, LANES), 0) * LANES + iota((8, LANES), 1)
    for j, out_ref in enumerate(out_refs):
        block = packed[j * rows : (j + 1) * rows]
        for t in range(tiles):
            out_ref[t * rows : (t + 1) * rows, :] = block[:, t * LANES : (t + 1) * LANES]
        mine = (slot_lane >= j * rows) & (slot_lane < (j + 1) * rows)
        out_ref[tiles * rows :, :] = jnp.where(mine, pos_tile, 0.0).astype(BF16)


def pack_ham_kernel(plan, size_ref, place_ref, ham_ref, *out_refs):
    slot_rows, cap = plan.slot_rows, plan.cap
    send = jnp.where(iota_f((slot_rows, cap), 0) == place_ref[...], 1.0, 0.0).astype(BF16)
    packed = dot(send, ham_ref[0])
    packed = jnp.where(iota((slot_rows, cap), 1) < size_ref[0], packed, 0.0).astype(BF16)
    for j, out_ref in enumerate(out_refs):
        out_ref[...] = packed[j * plan.rows : (j + 1) * plan.rows]


def ladder_kernel(
    plan, size_ref, factor_ref, swap_ref, place_ref, gen_ref, ham_ref,
    half_ref, trace_ref, pick_ref, swap_out_ref,
):
    cap, slot_rows = plan.cap, plan.slot_rows
    size = size_ref[0]
    inside = (iota((cap, cap), 0) < size) & (iota((cap, cap), 1) < size)
    factor = to_column(factor_ref[...])
    gen = jnp.where(inside, gen_ref[0].astype(F32), 0.0)
    ham = jnp.where(inside, ham_ref[0].astype(F32), 0.0)
    ladder = dot(gen.astype(BF16), (factor * ham).astype(BF16)) - dot(
        ham.astype(BF16), (factor * gen).astype(BF16)
    )
    half_ref[...] = 0.5 * ladder
    diagonal = jnp.where(iota((cap, cap), 0) == iota((cap, cap), 1), ladder, 0.0)
    trace = jnp.sum(jnp.sum(diagonal, axis=1, keepdims=True), axis=0, keepdims=True)
    trace_ref[...] = jnp.broadcast_to(trace, (1, LANES))
    place = place_ref[...]
    swap = swap_ref[...].astype(F32)
    swap_col = to_column(swap)
    place_col = to_column(place)
    place_swap = jnp.sum(
        jnp.where(iota_f((cap, cap), 1) == swap_col, place, 0.0), axis=1, keepdims=True
    )
    slot = iota_f((cap, slot_rows), 1)
    pick_ref[...] = (
        jnp.where(slot == place_col, 1.0, 0.0) - jnp.where(slot == place_swap, 1.0, 0.0)
    ).astype(BF16)
    swap_out_ref[...] = jnp.where(iota_f((cap, cap), 0) == swap, 1.0, 0.0).astype(BF16)


def load_gen(plan, refs, full_ref):
    rows = plan.rows
    for j, ref in enumerate(refs):
        for t in range(plan.tiles):
            full_ref[j * rows : (j + 1) * rows, t * LANES : (t + 1) * LANES] = ref[
                t * rows : (t + 1) * rows, :
            ]


def ph_gen_kernel(plan, *refs):
    cap, slot_rows, strip = plan.cap, plan.slot_rows, plan.strip
    blocks = refs[: plan.blocks]
    pos_ref, cols_ref, factor_ref = refs[plan.blocks : plan.blocks + 3]
    left_ref, scaled_ref, cols_out_ref, scale_ref, full_ref = refs[plan.blocks + 3 :]
    if plan.permutes:
        load_gen(plan, blocks, full_ref)
        tail = plan.tiles * plan.rows
        pos_tile = sum(ref[tail:, :].astype(F32) for ref in blocks)
        pos = jnp.concatenate([pos_tile[t : t + 1] for t in range(slot_rows // LANES)], axis=1)
        full = full_ref[...]
    else:
        pos = pos_ref[...]
        full = blocks[0][...]
    lane = iota((1, slot_rows), 1)
    raw = jnp.where(pos > 0, (pos - 1.0) * strip + lax.rem(lane, strip).astype(F32), -1.0)
    cols_col = to_column(cols_ref[...].astype(F32))
    column = jnp.sum(
        jnp.where(iota_f((cap, slot_rows), 0) == raw, cols_col, 0.0), axis=0, keepdims=True
    )
    column = jnp.where(pos > 0, column, -1.0)
    cols_hot = jnp.where(iota_f((cap, slot_rows), 0) == column, 1.0, 0.0).astype(BF16)
    cols_out_ref[...] = cols_hot
    raw_col = to_column(raw)
    scale = jnp.sum(
        jnp.where(iota_f((slot_rows, cap), 1) == raw_col, factor_ref[...], 0.0),
        axis=1,
        keepdims=True,
    )
    scale_ref[...] = scale
    left_ref[...] = dot(full, cols_hot).astype(BF16)
    scaled_ref[...] = (scale * full.astype(F32)).astype(BF16)


def ph_ham_kernel(plan, *refs):
    blocks = refs[: plan.blocks]
    left_gen_ref, scaled_gen_ref, cols_ref, scale_ref = refs[plan.blocks : plan.blocks + 4]
    out_refs = refs[plan.blocks + 4 : 2 * plan.blocks + 4]
    if plan.permutes:
        full = jnp.concatenate([ref[...] for ref in blocks], axis=0)
    else:
        full = blocks[0][...]
    left_ham = dot(full, cols_ref[...]).astype(BF16)
    scaled_ham = (scale_ref[...] * full.astype(F32)).astype(BF16)
    comm = dot(left_gen_ref[...], scaled_ham) - dot(left_ham, scaled_gen_ref[...])
    comm = comm.astype(BF16)
    for j, out_ref in enumerate(out_refs):
        out_ref[...] = comm[j * plan.rows : (j + 1) * plan.rows]


def flow_kernel(plan, *refs):
    cap = plan.cap
    blocks = refs[: plan.blocks]
    size_ref, half_ref, pick_ref, swap_ref, flow_ref = refs[plan.blocks :]
    if plan.permutes:
        full = jnp.concatenate([ref[...] for ref in blocks], axis=0)
    else:
        full = blocks[0][...]
    swapped = dot(full, swap_ref[...]).astype(BF16)
    anti = dot(pick_ref[...], full) - dot(pick_ref[...], swapped)
    size = size_ref[0]
    inside = (iota((cap, cap), 0) < size) & (iota((cap, cap), 1) < size)
    flow_ref[0] = jnp.where(inside, half_ref[...] + anti, 0.0)


def cost(flops, nbytes):
    return pl.CostEstimate(flops=flops, bytes_accessed=nbytes, transcendentals=0)


def butterfly_sum(value, axes):
    for axis in axes:
        n = lax.axis_size(axis)
        if n & (n - 1):
            value = lax.psum(value, axis)
            continue
        step = 1
        while step < n:
            value = value + lax.ppermute(value, axis, [(i, i ^ step) for i in range(n)])
            step *= 2
    return value


def on_device(
    eta_pp, ham_pp, pp_factor, ph_factor, channel_size, dest_dev, dest_sub, col_map, pair_swap
):
    cap = eta_pp.shape[1]
    plan = Plan(cap, dest_dev.shape[1], lax.axis_size("chan"))
    peers, slot_rows = plan.peers, plan.slot_rows
    me = lax.axis_index("chan").astype(jnp.int32)[None]
    square = 2 * cap * cap * slot_rows
    nbytes = 2 * cap * slot_rows
    shape = jax.ShapeDtypeStruct
    block_shape = (plan.rows, cap)

    def exchange(blocks):
        if plan.permutes:
            return [blocks[0]] + [
                lax.ppermute(blocks[j], "chan", [(i, i ^ j) for i in range(peers)])
                for j in range(1, peers)
            ]
        whole = blocks[0]
        whole = whole.reshape(peers, slot_rows // peers, whole.shape[1])
        whole = lax.all_to_all(whole, "chan", split_axis=0, concat_axis=0, tiled=True)
        return [whole.reshape(slot_rows, whole.shape[2])]

    place, pos, *gen_blocks = pl.pallas_call(
        functools.partial(pack_gen_kernel, plan),
        out_shape=[shape((1, cap), F32), shape((1, slot_rows), F32)]
        + [shape(plan.gen_shape, BF16)] * plan.blocks,
        in_specs=[SMEM, SMEM, VMEM, VMEM, VMEM],
        out_specs=[VMEM] * (2 + plan.blocks),
        cost_estimate=cost(square, 2 * nbytes),
        name="pack_gen",
    )(me, channel_size, dest_dev, dest_sub, eta_pp)
    ham_blocks = pl.pallas_call(
        functools.partial(pack_ham_kernel, plan),
        out_shape=[shape(block_shape, BF16)] * plan.blocks,
        in_specs=[SMEM, VMEM, VMEM],
        out_specs=[VMEM] * plan.blocks,
        cost_estimate=cost(square, 2 * nbytes),
        name="pack_ham",
    )(channel_size, place, ham_pp)
    gen_recv = exchange(gen_blocks)
    if not plan.permutes:
        pos = lax.all_to_all(
            pos.reshape(peers, slot_rows // peers), "chan", split_axis=0, concat_axis=0, tiled=True
        ).reshape(1, slot_rows)
    ham_recv = exchange(ham_blocks)

    half, trace, pick, swap_hot = pl.pallas_call(
        functools.partial(ladder_kernel, plan),
        out_shape=[
            shape((cap, cap), F32),
            shape((1, LANES), F32),
            shape((cap, slot_rows), BF16),
            shape((cap, cap), BF16),
        ],
        in_specs=[SMEM] + [VMEM] * 5,
        out_specs=[VMEM] * 4,
        cost_estimate=cost(2 * square, 4 * nbytes),
        name="ladder",
    )(channel_size, pp_factor, pair_swap, place, eta_pp, ham_pp)
    energy_flow = 0.25 * butterfly_sum(trace, ("grp", "chan"))[0, 0]

    left_gen, scaled_gen, cols_hot, scale = pl.pallas_call(
        functools.partial(ph_gen_kernel, plan),
        out_shape=[
            shape((slot_rows, slot_rows), BF16),
            shape((slot_rows, cap), BF16),
            shape((cap, slot_rows), BF16),
            shape((slot_rows, 1), F32),
        ],
        in_specs=[VMEM] * (plan.blocks + 3),
        out_specs=[VMEM] * 4,
        scratch_shapes=[pltpu.VMEM((slot_rows, cap), BF16)],
        cost_estimate=cost(square, 4 * nbytes),
        name="ph_gen",
    )(*gen_recv, pos, col_map, ph_factor)
    comm_blocks = pl.pallas_call(
        functools.partial(ph_ham_kernel, plan),
        out_shape=[shape(block_shape, BF16)] * plan.blocks,
        in_specs=[VMEM] * (plan.blocks + 4),
        out_specs=[VMEM] * plan.blocks,
        cost_estimate=cost(3 * square, 5 * nbytes),
        name="ph_ham",
    )(*ham_recv, left_gen, scaled_gen, cols_hot, scale)
    back_blocks = exchange(comm_blocks)
    flow = pl.pallas_call(
        functools.partial(flow_kernel, plan),
        out_shape=shape((1, cap, cap), F32),
        in_specs=[VMEM] * plan.blocks + [SMEM, VMEM, VMEM, VMEM],
        out_specs=VMEM,
        cost_estimate=cost(3 * square, 7 * nbytes),
        name="flow",
    )(*back_blocks, channel_size, half, pick, swap_hot)
    return (flow, energy_flow)


def solution(mesh):
    in_specs = (
        P(("chan", "grp"), None, None),
        P(("chan", "grp"), None, None),
        P(("chan", "grp"), None),
        P(("chan", "grp"), None),
        P(("chan", "grp")),
        P(("chan", "grp"), None),
        P(("chan", "grp"), None),
        P(("chan", "grp"), None),
        P(("chan", "grp"), None),
    )
    out_specs = (P(("chan", "grp"), None, None), P())
    return jax.shard_map(
        on_device, mesh=mesh, in_specs=in_specs, out_specs=out_specs, check_vma=False
    )
```
